32 devices in a mesh: lsec: 4 (over y, x), rsec: 8 (over z, core).
Axes of the slice: x: 2, y: 2, z: 4, core: 2. Of those that a mesh axis runs over, the one named last changes fastest.
Arguments:
- psi: bfloat16 [16, 16, 256, 256], P('lsec', 'rsec'), may hold values from -6 to 6
- left_env: bfloat16 [16, 4, 256, 256], P('lsec'), may hold values from -0.375 to 0.375
- right_env: bfloat16 [16, 4, 256, 256], P('rsec'), may hold values from -0.1875 to 0.1875
- energies: float32 [16, 16], P('lsec', 'rsec'), may hold values from 0.5 to 3
- coef_num: int32 [2], replicated, may hold values from 3 to 9
- coef_den: int32 [2], replicated, may hold values from 4 to 8
Outputs:
- vector_out: bfloat16 [16, 16, 256, 256], P('lsec', 'rsec')
- ritz: float32 [3], replicated
The draws below stay inside these ranges and needn't reach their ends.
All inputs are finite; a program needn't handle non-finite values.
Results may differ from the reference program's by a relative error of at most 0.015.
Values may be sent and summed in bfloat16 or wider, within the bound.
A program may use at most 64 MiB of HBM per device.

```python
import jax
import jax.numpy as jnp
from jax import lax

B = 256
DIAG = 2
HOPS = 1
ITERS = 3
TERMS = 4
NA = 16
NB = 16


def block_levels(rng, dims, shards, smallest, top_value):
    loudness, own = 1.0, jax.random.fold_in(rng, 6)
    for dim, parts in shards:
        draws = jnp.exp(jax.random.uniform(jax.random.fold_in(own, dim), (parts,), jnp.float32, smallest / len(shards), top_value / len(shards)))
        loudness = loudness * jnp.repeat(draws, dims[dim] // parts).reshape([-1 if axis == dim else 1 for axis in range(len(dims))])
    return loudness


def centred(own_key, shape, width, bound, shards=(), kind=jnp.bfloat16):
    entries = jax.random.normal(own_key, shape, jnp.float32) * width
    if len(shards) > 0:
        entries = block_levels(own_key, shape, shards, -0.22, 0.18) * entries
    return jnp.clip(entries, min=-bound, max=bound).astype(kind)


def setup_inputs(seed: int = 0) -> dict:
    arg_keys = jax.random.split(jax.random.key(seed), 7)
    psi = centred(arg_keys[0], (NA, NB, B, B), 1.0, 6.0, ((0, 4), (1, 8)))
    left_env = centred(arg_keys[1], (NA, TERMS, B, B), B ** -0.5, 0.375, ((0, 4),))
    right_env = centred(arg_keys[2], (NB, TERMS, B, B), (B * TERMS) ** -0.5, 0.1875, ((0, 8),))
    energies = jnp.clip(0.5 + 2.5 * jax.random.uniform(arg_keys[3], (NA, NB), jnp.float32) ** block_levels(arg_keys[3], (NA, NB), ((0, 4), (1, 8)), -0.2, 0.2), 0.5, 3.0)
    coef_num = jax.random.randint(arg_keys[4], (ITERS - 1,), 3, 10).astype(jnp.int32)
    coef_den = jax.random.randint(arg_keys[5], (ITERS - 1,), 4, 9).astype(jnp.int32)
    return {"psi": psi, "left_env": left_env, "right_env": right_env, "energies": energies, "coef_num": coef_num, "coef_den": coef_den}


eps = 1e-06

def matvec(vec, left_env, right_env, energies):
    vals = vec.astype(jnp.float32)
    padded = jnp.pad(vals, ((1, 1), (1, 1), (0, 0), (0, 0)))
    plus_blocks = padded[:-2, 2:]
    minus_blocks = padded[2:, :-2]
    total = energies[:, :, None, None] * vals
    left_all = left_env.astype(jnp.float32)
    right_all = right_env.astype(jnp.float32)
    for term in range(DIAG + 2 * HOPS):
        if term < DIAG:
            source = vals
        elif term < DIAG + HOPS:
            source = plus_blocks
        else:
            source = minus_blocks
        inner = jnp.einsum('aij,abjk->abik', left_all[:, term], source).astype(jnp.bfloat16)
        total = total + jnp.einsum('abik,blk->abil', inner.astype(jnp.float32), right_all[:, term])
    return total

def reference(psi, left_env, right_env, energies, coef_num, coef_den):
    count = 1.0 / float(psi.size)
    start_vals = psi.astype(jnp.float32)
    start = jnp.sum(start_vals * start_vals) * count
    vec = (start_vals * lax.rsqrt(start + eps)).astype(jnp.bfloat16)
    previous = jnp.zeros(psi.shape, jnp.float32)
    thetas = []
    for step in range(ITERS):
        sigma = matvec(vec, left_env, right_env, energies)
        vals = vec.astype(jnp.float32)
        theta = jnp.sum(vals * sigma) * count
        thetas.append(theta)
        if step == 0:
            coef = jnp.float32(0.0)
        else:
            coef = coef_num[step - 1].astype(jnp.float32) / coef_den[step - 1].astype(jnp.float32)
        resid = sigma - theta * vals - coef * previous
        norm_sq = jnp.sum(resid * resid) * count
        previous = vals
        vec = (resid * lax.rsqrt(norm_sq + eps)).astype(jnp.bfloat16)
    return (vec, jnp.stack(thetas))
```

```python
import functools

import jax
import jax.numpy as jnp
from jax import lax
from jax.experimental import pallas as pl
from jax.experimental.pallas import tpu as pltpu
from jax.sharding import PartitionSpec as P

DIAG = 2
HOPS = 1
TERMS = DIAG + 2 * HOPS
ITERS = 3
eps = 1e-06
SHIFT = 1.75
GRAMS = 16
MESH = pl.DeviceIdType.MESH


def gram_row(i, j):
    return j * (j + 1) // 2 + i


def kernel(
    nl, nr, count,
    psi_hbm, left_hbm, right_hbm, energies, coef_num, coef_den,
    out_hbm, ritz,
    q, left, right, right_t, acc, out_v, rows, cols,
    send_sem, recv_sem, in_sem, rsend, rrecv, csend, crecv,
):
    na, nb, size, _ = psi_hbm.shape
    me_l, me_r = lax.axis_index("lsec"), lax.axis_index("rsec")
    has_lo_l, has_hi_l = me_l > 0, me_l < nl - 1
    has_lo_r, has_hi_r = me_r > 0, me_r < nr - 1
    up_dn = jnp.logical_and(has_hi_l, has_lo_r)
    dn_up = jnp.logical_and(has_lo_l, has_hi_r)

    loads = [
        pltpu.make_async_copy(psi_hbm, q.at[0, 1 : na + 1, 1 : nb + 1], in_sem.at[0]),
        pltpu.make_async_copy(right_hbm, right, in_sem.at[1]),
        pltpu.make_async_copy(left_hbm, left, in_sem.at[2]),
    ]
    for load in loads:
        load.start()

    barrier = pltpu.get_barrier_semaphore()

    def greet(target):
        pl.semaphore_signal(barrier, inc=1, device_id=target, device_id_type=MESH)

    for step in range(1, nr):
        greet((me_l, lax.rem(me_r + step, nr)))
    for step in range(1, nl):
        greet((lax.rem(me_l + step, nl), me_r))

    @pl.when(up_dn)
    def _():
        greet((me_l + 1, me_r - 1))

    @pl.when(dn_up)
    def _():
        greet((me_l - 1, me_r + 1))

    def hops(k):
        lo_l, hi_l, lo_r, hi_r = me_l - 1, me_l + 1, me_r - 1, me_r + 1
        here = q.at[k]
        plan = (
            (has_hi_l, has_lo_l, here.at[na, 2 : nb + 1], here.at[0, 2 : nb + 1], (hi_l, me_r)),
            (up_dn, dn_up, here.at[na, 1], here.at[0, nb + 1], (hi_l, lo_r)),
            (has_lo_l, has_hi_l, here.at[1, 1:nb], here.at[na + 1, 1:nb], (lo_l, me_r)),
            (dn_up, up_dn, here.at[1, nb], here.at[na + 1, 0], (lo_l, hi_r)),
            (has_lo_r, has_hi_r, here.at[1:na, 1], here.at[1:na, nb + 1], (me_l, lo_r)),
            (has_hi_r, has_lo_r, here.at[2 : na + 1, nb], here.at[2 : na + 1, 0], (me_l, hi_r)),
        )

        def copy(n):
            return pltpu.make_async_remote_copy(
                src_ref=plan[n][2], dst_ref=plan[n][3],
                send_sem=send_sem.at[k, n], recv_sem=recv_sem.at[k, n],
                device_id=plan[n][4], device_id_type=MESH,
            )

        return plan, copy

    def send(k, which):
        plan, copy = hops(k)
        for n in which:
            pl.when(plan[n][0])(lambda n=n: copy(n).start())

    def receive(k, which):
        plan, copy = hops(k)
        for n in which:
            pl.when(plan[n][1])(lambda n=n: copy(n).wait_recv())

    def clear(missing, slots):
        @pl.when(jnp.logical_not(missing))
        def _():
            for k in range(ITERS):
                for i, j in slots:
                    q[k, i, j] = jnp.zeros((size, size), q.dtype)

    clear(has_lo_l, [(0, j) for j in range(2, nb + 1)])
    clear(dn_up, [(0, nb + 1)])
    clear(has_hi_l, [(na + 1, j) for j in range(1, nb)])
    clear(up_dn, [(na + 1, 0)])
    clear(has_hi_r, [(i, nb + 1) for i in range(1, na)])
    clear(has_lo_r, [(i, 0) for i in range(2, na + 1)])

    rows[me_r] = jnp.zeros(rows.shape[1:], jnp.float32)
    partners = nr - 1 + nl - 1
    partners = partners + up_dn.astype(jnp.int32) + dn_up.astype(jnp.int32)
    loads[0].wait()
    pl.semaphore_wait(barrier, partners)
    send(0, range(6))
    loads[1].wait()
    for j in range(nb):
        for t in range(TERMS):
            right_t[j, t] = right[j, t].T
    loads[2].wait()

    def term(i, j, t, source):
        inner = jnp.dot(left[i, t], source, preferred_element_type=jnp.float32)
        return jnp.dot(
            inner.astype(jnp.bfloat16), right_t[j, t], preferred_element_type=jnp.float32
        )

    def gram(i, j):
        total = jnp.zeros((size, size), jnp.float32)
        for a in range(1, na + 1):
            for b in range(1, nb + 1):
                total += q[i, a, b].astype(jnp.float32) * q[j, a, b].astype(jnp.float32)
        folded = jnp.sum(total, axis=0, keepdims=True)
        part = folded[:, 0:128]
        for lane in range(128, size, 128):
            part = part + folded[:, lane : lane + 128]
        rows[me_r, pl.ds(gram_row(i, j), 1), :] = part

    gram(0, 0)

    def is_local(t, i, j):
        if t < DIAG:
            return True
        if t < DIAG + HOPS:
            return i >= 1 and j + 1 < nb
        return i + 1 < na and j >= 1

    def offset(t):
        return 0 if t < DIAG else (1 if t < DIAG + HOPS else -1)

    def source_of(k, t, i, j):
        return q[k, i + 1 - offset(t), j + 1 + offset(t)]

    def step(k, carry):
        for i in range(na):
            for j in range(nb):
                own = q[k, i + 1, j + 1]
                total = (energies[i, j] - SHIFT) * own.astype(jnp.float32)
                for t in range(TERMS):
                    if is_local(t, i, j):
                        total += term(i, j, t, source_of(k, t, i, j))
                acc[i, j] = total

        def finish(i, j, ts):
            total = acc[i, j]
            for t in ts:
                total += term(i, j, t, source_of(k, t, i, j))
            acc[i, j] = total
            q[k + 1, i + 1, j + 1] = total.astype(jnp.bfloat16)

        corners = ((0, 0), (na - 1, nb - 1), (0, nb - 1), (na - 1, 0))
        receive(k, (5, 4))
        for i in range(na):
            for j in range(nb):
                if (i, j) not in corners:
                    finish(i, j, [t for t in range(DIAG, TERMS) if not is_local(t, i, j)])
        receive(k, (0, 2, 1, 3))
        for i, j in corners:
            finish(i, j, [t for t in range(DIAG, TERMS) if not is_local(t, i, j)])

        @pl.when(k + 1 < ITERS)
        def _():
            send(k + 1, range(6))

        lax.fori_loop(0, k + 2, lambda i, c: (gram(i, k + 1), c)[1], 0)
        return carry

    lax.fori_loop(0, ITERS, step, 0)

    def spread(slots, me, parts, to, ssem, rsem):
        def copy(n, slot):
            return pltpu.make_async_remote_copy(
                src_ref=slots.at[slot], dst_ref=slots.at[slot],
                send_sem=ssem.at[n], recv_sem=rsem.at[slot],
                device_id=to(lax.rem(me + n, parts)), device_id_type=MESH,
            )

        for n in range(1, parts):
            copy(n, me).start()
        for n in range(1, parts):
            copy(n, lax.rem(me + n, parts)).wait_recv()
        for n in range(1, parts):
            copy(n, me).wait_send()
        total = slots[0]
        for n in range(1, parts):
            total = total + slots[n]
        return total

    cols[me_l] = spread(rows, me_r, nr, lambda r: (me_l, r), rsend, rrecv)
    sums = spread(cols, me_l, nl, lambda l: (l, me_r), csend, crecv)
    sums = jnp.sum(sums, axis=1, keepdims=True) * count

    def mean(i, j):
        row = gram_row(min(i, j), max(i, j))
        return sums[row : row + 1, :]

    def product(x, y):
        total = jnp.zeros((1, 1), jnp.float32)
        for i in range(ITERS + 1):
            for j in range(ITERS + 1):
                if x[i] is not None and y[j] is not None:
                    total = total + x[i] * y[j] * mean(i, j)
        return total

    def plus(x, y):
        return y if x is None else (x if y is None else x + y)

    def scaled(s, x):
        return [None if part is None else s * part for part in x]

    def combine(*lists):
        return [functools.reduce(plus, parts) for parts in zip(*lists)]

    vec = [lax.rsqrt(mean(0, 0) + eps)] + [None] * ITERS
    previous = [None] * (ITERS + 1)
    for k in range(ITERS):
        sigma = combine([None] + vec[:-1], scaled(SHIFT, vec))
        theta = product(vec, sigma)
        resid = combine(sigma, scaled(-theta, vec))
        if k > 0:
            coef = jnp.full((1, 1), coef_num[k - 1].astype(jnp.float32)) / jnp.full(
                (1, 1), coef_den[k - 1].astype(jnp.float32)
            )
            resid = combine(resid, scaled(-coef, previous))
        ritz[k] = theta[0, 0]
        previous = vec
        vec = scaled(lax.rsqrt(product(resid, resid) + eps), resid)

    stores = []
    for i in range(na):
        for j in range(nb):
            total = acc[i, j] * vec[ITERS]
            for n in range(ITERS):
                total += q[n, i + 1, j + 1].astype(jnp.float32) * vec[n]
            out_v[i, j] = total.astype(jnp.bfloat16)
        stores.append(pltpu.make_async_copy(out_v.at[i], out_hbm.at[i], in_sem.at[i]))
        stores[-1].start()

    for k in range(ITERS):
        plan, copy = hops(k)
        for n in range(6):
            pl.when(plan[n][0])(lambda n=n: copy(n).wait_send())
    for store in stores:
        store.wait()


def per_device(nl, nr, psi, left_env, right_env, energies, coef_num, coef_den):
    na, nb, size, _ = psi.shape
    count = 1.0 / float(psi.size * nl * nr)
    anywhere = pl.BlockSpec(memory_space=pl.ANY)
    smem = pl.BlockSpec(memory_space=pltpu.SMEM)
    dma = pltpu.SemaphoreType.DMA
    return pl.pallas_call(
        functools.partial(kernel, nl, nr, count),
        out_shape=(
            jax.ShapeDtypeStruct(psi.shape, jnp.bfloat16),
            jax.ShapeDtypeStruct((ITERS,), jnp.float32),
        ),
        in_specs=[anywhere] * 3 + [smem] * 3,
        out_specs=(anywhere, smem),
        scratch_shapes=[
            pltpu.VMEM((ITERS + 1, na + 2, nb + 2, size, size), jnp.bfloat16),
            pltpu.VMEM(left_env.shape, jnp.bfloat16),
            pltpu.VMEM(right_env.shape, jnp.bfloat16),
            pltpu.VMEM(right_env.shape, jnp.bfloat16),
            pltpu.VMEM(psi.shape, jnp.float32),
            pltpu.VMEM(psi.shape, jnp.bfloat16),
            pltpu.VMEM((nr, GRAMS, 128), jnp.float32),
            pltpu.VMEM((nl, GRAMS, 128), jnp.float32),
            dma((ITERS, 6)),
            dma((ITERS, 6)),
            dma((max(3, na),)),
            dma((nr,)),
            dma((nr,)),
            dma((nl,)),
            dma((nl,)),
        ],
        compiler_params=pltpu.CompilerParams(
            collective_id=0, has_side_effects=True, vmem_limit_bytes=60000000
        ),
    )(psi, left_env, right_env, energies, coef_num, coef_den)


def solution(mesh):
    in_specs = (
        P("lsec", "rsec", None, None),
        P("lsec", None, None, None),
        P("rsec", None, None, None),
        P("lsec", "rsec"),
        P(),
        P(),
    )
    out_specs = (P("lsec", "rsec", None, None), P())
    body = functools.partial(per_device, mesh.shape["lsec"], mesh.shape["rsec"])
    return jax.shard_map(
        body, mesh=mesh, in_specs=in_specs, out_specs=out_specs, check_vma=False
    )
```

```python
import functools

import jax
import jax.numpy as jnp
from jax import lax
from jax.experimental import pallas as pl
from jax.experimental.pallas import tpu as pltpu
from jax.sharding import PartitionSpec as P

DIAG = 2
HOPS = 1
TERMS = DIAG + 2 * HOPS
ITERS = 3
eps = 1e-06
SHIFT = 1.75
GRAMS = 16
MESH = pl.DeviceIdType.MESH


def gram_row(i, j):
    return j * (j + 1) // 2 + i


def kernel(
    nl, nr, count,
    psi_hbm, left_hbm, right_hbm, energies, coef_num, coef_den,
    out_hbm, ritz,
    q, stage, left, right, right_t, acc, out_v, rows, cols,
    send_sem, recv_sem, in_sem, rsend, rrecv, csend, crecv,
):
    na, nb, size, _ = psi_hbm.shape
    me_l, me_r = lax.axis_index("lsec"), lax.axis_index("rsec")
    has_lo_l, has_hi_l = me_l > 0, me_l < nl - 1
    has_lo_r, has_hi_r = me_r > 0, me_r < nr - 1
    up_dn = jnp.logical_and(has_hi_l, has_lo_r)
    dn_up = jnp.logical_and(has_lo_l, has_hi_r)
    odd = lax.rem(me_l, 2) == 1
    even = jnp.logical_not(odd)
    via_hi = jnp.logical_and(up_dn, jnp.logical_and(odd, me_l + 2 < nl))
    via_lo = jnp.logical_and(dn_up, jnp.logical_and(even, me_l >= 2))
    relay_dn = jnp.logical_and(jnp.logical_and(odd, me_l >= 2), has_lo_r)
    relay_up = jnp.logical_and(jnp.logical_and(even, me_l + 2 < nl), has_hi_r)
    up_up = jnp.logical_and(even, jnp.logical_and(has_hi_l, has_hi_r))
    dn_dn = jnp.logical_and(odd, has_lo_r)

    loads = [
        pltpu.make_async_copy(psi_hbm, q.at[0, 1 : na + 1, 1 : nb + 1], in_sem.at[0]),
        pltpu.make_async_copy(right_hbm, right, in_sem.at[1]),
        pltpu.make_async_copy(left_hbm, left, in_sem.at[2]),
    ]
    for load in loads:
        load.start()

    barrier = pltpu.get_barrier_semaphore()

    def greet(target):
        pl.semaphore_signal(barrier, inc=1, device_id=target, device_id_type=MESH)

    for step in range(1, nr):
        greet((me_l, lax.rem(me_r + step, nr)))
    for step in range(1, nl):
        greet((lax.rem(me_l + step, nl), me_r))

    @pl.when(up_dn)
    def _():
        greet((me_l + 1, me_r - 1))

    @pl.when(dn_up)
    def _():
        greet((me_l - 1, me_r + 1))

    @pl.when(up_up)
    def _():
        greet((me_l + 1, me_r + 1))

    @pl.when(dn_dn)
    def _():
        greet((me_l - 1, me_r - 1))

    def hops(k):
        lo_l, hi_l, lo_r, hi_r = me_l - 1, me_l + 1, me_r - 1, me_r + 1
        here = q.at[k]
        up_ref, dn_ref = here.at[na, 1], here.at[1, nb]
        up_dst, dn_dst = here.at[0, nb + 1], here.at[na + 1, 0]
        up_stage, dn_stage = stage.at[k, 0], stage.at[k, 1]
        no = jnp.logical_not
        return (
            (has_hi_l, has_lo_l, here.at[na, 2 : nb + 1], here.at[0, 2 : nb + 1], (hi_l, me_r), 0, 0),
            (jnp.logical_and(up_dn, no(via_hi)), dn_up, up_ref, up_dst, (hi_l, lo_r), 1, 1),
            (has_lo_l, has_hi_l, here.at[1, 1:nb], here.at[na + 1, 1:nb], (lo_l, me_r), 2, 2),
            (jnp.logical_and(dn_up, no(via_lo)), up_dn, dn_ref, dn_dst, (lo_l, hi_r), 3, 3),
            (has_lo_r, has_hi_r, here.at[2:na, 1], here.at[2:na, nb + 1], (me_l, lo_r), 4, 4),
            (has_hi_r, has_lo_r, here.at[2:na, nb], here.at[2:na, 0], (me_l, hi_r), 5, 5),
            (has_lo_r, has_hi_r, here.at[1, 1], here.at[1, nb + 1], (me_l, lo_r), 6, 6),
            (has_hi_r, has_lo_r, here.at[na, nb], here.at[na, 0], (me_l, hi_r), 7, 7),
            (via_hi, relay_dn, up_ref, up_stage, (me_l + 2, me_r), 1, 8),
            (via_lo, relay_up, dn_ref, dn_stage, (me_l - 2, me_r), 3, 9),
            (relay_dn, None, up_stage, up_dst, (lo_l, lo_r), 8, 1),
            (relay_up, None, dn_stage, dn_dst, (hi_l, hi_r), 9, 3),
        )

    def copy(k, n):
        _, _, src, dst, target, ssem, rsem = hops(k)[n]
        return pltpu.make_async_remote_copy(
            src_ref=src, dst_ref=dst,
            send_sem=send_sem.at[k, ssem], recv_sem=recv_sem.at[k, rsem],
            device_id=target, device_id_type=MESH,
        )

    def send(k, which):
        for n in which:
            pl.when(hops(k)[n][0])(lambda n=n: copy(k, n).start())

    def receive(k, which):
        for n in which:
            pl.when(hops(k)[n][1])(lambda n=n: copy(k, n).wait_recv())

    def forward(k):
        receive(k, (8, 9))
        send(k, (10, 11))

    def clear(missing, slots):
        @pl.when(jnp.logical_not(missing))
        def _():
            for k in range(ITERS):
                for i, j in slots:
                    q[k, i, j] = jnp.zeros((size, size), q.dtype)

    clear(has_lo_l, [(0, j) for j in range(2, nb + 1)])
    clear(dn_up, [(0, nb + 1)])
    clear(has_hi_l, [(na + 1, j) for j in range(1, nb)])
    clear(up_dn, [(na + 1, 0)])
    clear(has_hi_r, [(i, nb + 1) for i in range(1, na)])
    clear(has_lo_r, [(i, 0) for i in range(2, na + 1)])

    rows[me_r] = jnp.zeros(rows.shape[1:], jnp.float32)
    partners = nr - 1 + nl - 1
    for other in (up_dn, dn_up, up_up, dn_dn):
        partners = partners + other.astype(jnp.int32)
    loads[0].wait()
    pl.semaphore_wait(barrier, partners)
    send(0, (8, 9, 0, 2, 1, 3, 4, 5, 6, 7))
    loads[1].wait()
    for j in range(nb):
        for t in range(TERMS):
            right_t[j, t] = right[j, t].T
    loads[2].wait()

    def term(i, j, t, source):
        inner = jnp.dot(left[i, t], source, preferred_element_type=jnp.float32)
        return jnp.dot(
            inner.astype(jnp.bfloat16), right_t[j, t], preferred_element_type=jnp.float32
        )

    def gram(i, j):
        total = jnp.zeros((size, size), jnp.float32)
        for a in range(1, na + 1):
            for b in range(1, nb + 1):
                total += q[i, a, b].astype(jnp.float32) * q[j, a, b].astype(jnp.float32)
        folded = jnp.sum(total, axis=0, keepdims=True)
        part = folded[:, 0:128]
        for lane in range(128, size, 128):
            part = part + folded[:, lane : lane + 128]
        rows[me_r, pl.ds(gram_row(i, j), 1), :] = part

    gram(0, 0)

    def is_local(t, i, j):
        if t < DIAG:
            return True
        if t < DIAG + HOPS:
            return i >= 1 and j + 1 < nb
        return i + 1 < na and j >= 1

    def offset(t):
        return 0 if t < DIAG else (1 if t < DIAG + HOPS else -1)

    def source_of(k, t, i, j):
        return q[k, i + 1 - offset(t), j + 1 + offset(t)]

    def step(k, carry):
        for i in range(na):
            for j in range(nb):
                own = q[k, i + 1, j + 1]
                total = (energies[j, i] - SHIFT) * own.astype(jnp.float32)
                for t in range(TERMS):
                    if is_local(t, i, j):
                        total += term(i, j, t, source_of(k, t, i, j))
                acc[i, j] = total

        def finish(i, j, ts):
            total = acc[i, j]
            for t in ts:
                total += term(i, j, t, source_of(k, t, i, j))
            acc[i, j] = total
            q[k + 1, i + 1, j + 1] = total.astype(jnp.bfloat16)

        def remote(i, j):
            return [t for t in range(DIAG, TERMS) if not is_local(t, i, j)]

        def onward(which):
            pl.when(k + 1 < ITERS)(lambda: send(k + 1, which))

        forward(k)
        receive(k, (4, 5, 6, 7))
        for i in range(1, na - 1):
            for j in range(nb):
                finish(i, j, remote(i, j))
        onward((4, 5))
        receive(k, (0,))
        for j in range(nb - 1):
            finish(0, j, remote(0, j))
        onward((2, 6))
        receive(k, (2,))
        for j in range(1, nb):
            finish(na - 1, j, remote(na - 1, j))
        onward((0, 7))
        receive(k, (1,))
        finish(0, nb - 1, remote(0, nb - 1))
        onward((9, 3))
        receive(k, (3,))
        finish(na - 1, 0, remote(na - 1, 0))
        onward((8, 1))

        lax.fori_loop(0, k + 2, lambda i, c: (gram(i, k + 1), c)[1], 0)
        return carry

    lax.fori_loop(0, ITERS, step, 0)

    def spread(slots, me, parts, to, ssem, rsem):
        def copy(n, slot):
            return pltpu.make_async_remote_copy(
                src_ref=slots.at[slot], dst_ref=slots.at[slot],
                send_sem=ssem.at[n], recv_sem=rsem.at[slot],
                device_id=to(lax.rem(me + n, parts)), device_id_type=MESH,
            )

        for n in range(1, parts):
            copy(n, me).start()
        for n in range(1, parts):
            copy(n, lax.rem(me + n, parts)).wait_recv()
        for n in range(1, parts):
            copy(n, me).wait_send()
        total = slots[0]
        for n in range(1, parts):
            total = total + slots[n]
        return total

    cols[me_l] = spread(rows, me_r, nr, lambda r: (me_l, r), rsend, rrecv)
    sums = spread(cols, me_l, nl, lambda l: (l, me_r), csend, crecv)
    sums = jnp.sum(sums, axis=1, keepdims=True) * count

    def mean(i, j):
        row = gram_row(min(i, j), max(i, j))
        return sums[row : row + 1, :]

    def product(x, y):
        total = jnp.zeros((1, 1), jnp.float32)
        for i in range(ITERS + 1):
            for j in range(ITERS + 1):
                if x[i] is not None and y[j] is not None:
                    total = total + x[i] * y[j] * mean(i, j)
        return total

    def plus(x, y):
        return y if x is None else (x if y is None else x + y)

    def scaled(s, x):
        return [None if part is None else s * part for part in x]

    def combine(*lists):
        return [functools.reduce(plus, parts) for parts in zip(*lists)]

    vec = [lax.rsqrt(mean(0, 0) + eps)] + [None] * ITERS
    previous = [None] * (ITERS + 1)
    for k in range(ITERS):
        sigma = combine([None] + vec[:-1], scaled(SHIFT, vec))
        theta = product(vec, sigma)
        resid = combine(sigma, scaled(-theta, vec))
        if k > 0:
            coef = jnp.full((1, 1), coef_num[k - 1].astype(jnp.float32)) / jnp.full(
                (1, 1), coef_den[k - 1].astype(jnp.float32)
            )
            resid = combine(resid, scaled(-coef, previous))
        ritz[k] = theta[0, 0]
        previous = vec
        vec = scaled(lax.rsqrt(product(resid, resid) + eps), resid)

    stores = []
    for i in range(na):
        for j in range(nb):
            total = acc[i, j] * vec[ITERS]
            for n in range(ITERS):
                total += q[n, i + 1, j + 1].astype(jnp.float32) * vec[n]
            out_v[i, j] = total.astype(jnp.bfloat16)
        stores.append(pltpu.make_async_copy(out_v.at[i], out_hbm.at[i], in_sem.at[i]))
        stores[-1].start()

    for k in range(ITERS):
        for n in range(12):
            pl.when(hops(k)[n][0])(lambda k=k, n=n: copy(k, n).wait_send())
    for store in stores:
        store.wait()


def per_device(nl, nr, psi, left_env, right_env, energies, coef_num, coef_den):
    na, nb, size, _ = psi.shape
    count = 1.0 / float(psi.size * nl * nr)
    anywhere = pl.BlockSpec(memory_space=pl.ANY)
    smem = pl.BlockSpec(memory_space=pltpu.SMEM)
    dma = pltpu.SemaphoreType.DMA
    return pl.pallas_call(
        functools.partial(kernel, nl, nr, count),
        out_shape=(
            jax.ShapeDtypeStruct(psi.shape, jnp.bfloat16),
            jax.ShapeDtypeStruct((ITERS,), jnp.float32),
        ),
        in_specs=[anywhere] * 3 + [smem] * 3,
        out_specs=(anywhere, smem),
        scratch_shapes=[
            pltpu.VMEM((ITERS + 1, na + 2, nb + 2, size, size), jnp.bfloat16),
            pltpu.VMEM((ITERS, 2, size, size), jnp.bfloat16),
            pltpu.VMEM(left_env.shape, jnp.bfloat16),
            pltpu.VMEM(right_env.shape, jnp.bfloat16),
            pltpu.VMEM(right_env.shape, jnp.bfloat16),
            pltpu.VMEM(psi.shape, jnp.float32),
            pltpu.VMEM(psi.shape, jnp.bfloat16),
            pltpu.VMEM((nr, GRAMS, 128), jnp.float32),
            pltpu.VMEM((nl, GRAMS, 128), jnp.float32),
            dma((ITERS, 10)),
            dma((ITERS, 10)),
            dma((max(3, na),)),
            dma((nr,)),
            dma((nr,)),
            dma((nl,)),
            dma((nl,)),
        ],
        compiler_params=pltpu.CompilerParams(
            collective_id=0, has_side_effects=True, vmem_limit_bytes=60000000
        ),
    )(psi, left_env, right_env, energies.T, coef_num, coef_den)


def solution(mesh):
    in_specs = (
        P("lsec", "rsec", None, None),
        P("lsec", None, None, None),
        P("rsec", None, None, None),
        P("lsec", "rsec"),
        P(),
        P(),
    )
    out_specs = (P("lsec", "rsec", None, None), P())
    body = functools.partial(per_device, mesh.shape["lsec"], mesh.shape["rsec"])
    return jax.shard_map(
        body, mesh=mesh, in_specs=in_specs, out_specs=out_specs, check_vma=False
    )
```

```python
import functools

import jax
import jax.numpy as jnp
from jax import lax
from jax.experimental import pallas as pl
from jax.experimental.pallas import tpu as pltpu
from jax.sharding import PartitionSpec as P

DIAG = 2
HOPS = 1
TERMS = DIAG + 2 * HOPS
ITERS = 3
eps = 1e-06
SHIFT = 1.75
GRAMS = 16
MESH = pl.DeviceIdType.MESH


def gram_row(i, j):
    return j * (j + 1) // 2 + i


def kernel(
    nl, nr, count,
    psi_hbm, left_hbm, right_hbm, energies, coef_num, coef_den,
    out_hbm, ritz,
    q, stage, left, right, right_t, acc, out_v, local, rows, cols,
    send_sem, recv_sem, in_sem, rsend, rrecv, csend, crecv,
):
    na, nb, size, _ = psi_hbm.shape
    me_l, me_r = lax.axis_index("lsec"), lax.axis_index("rsec")
    has_lo_l, has_hi_l = me_l > 0, me_l < nl - 1
    has_lo_r, has_hi_r = me_r > 0, me_r < nr - 1
    up_dn = jnp.logical_and(has_hi_l, has_lo_r)
    dn_up = jnp.logical_and(has_lo_l, has_hi_r)
    odd = lax.rem(me_l, 2) == 1
    even = jnp.logical_not(odd)
    via_hi = jnp.logical_and(up_dn, jnp.logical_and(odd, me_l + 2 < nl))
    via_lo = jnp.logical_and(dn_up, jnp.logical_and(even, me_l >= 2))
    relay_dn = jnp.logical_and(jnp.logical_and(odd, me_l >= 2), has_lo_r)
    relay_up = jnp.logical_and(jnp.logical_and(even, me_l + 2 < nl), has_hi_r)
    up_up = jnp.logical_and(even, jnp.logical_and(has_hi_l, has_hi_r))
    dn_dn = jnp.logical_and(odd, has_lo_r)

    loads = [
        pltpu.make_async_copy(psi_hbm, q.at[0, 1 : na + 1, 1 : nb + 1], in_sem.at[0]),
        pltpu.make_async_copy(right_hbm, right, in_sem.at[1]),
        pltpu.make_async_copy(left_hbm, left, in_sem.at[2]),
    ]
    for load in loads:
        load.start()

    barrier = pltpu.get_barrier_semaphore()

    def greet(target):
        pl.semaphore_signal(barrier, inc=1, device_id=target, device_id_type=MESH)

    for step in range(1, nr):
        greet((me_l, lax.rem(me_r + step, nr)))
    for step in range(1, nl):
        greet((lax.rem(me_l + step, nl), me_r))

    @pl.when(up_dn)
    def _():
        greet((me_l + 1, me_r - 1))

    @pl.when(dn_up)
    def _():
        greet((me_l - 1, me_r + 1))

    @pl.when(up_up)
    def _():
        greet((me_l + 1, me_r + 1))

    @pl.when(dn_dn)
    def _():
        greet((me_l - 1, me_r - 1))

    def hops(k):
        lo_l, hi_l, lo_r, hi_r = me_l - 1, me_l + 1, me_r - 1, me_r + 1
        here = q.at[k]
        up_ref, dn_ref = here.at[na, 1], here.at[1, nb]
        up_dst, dn_dst = here.at[0, nb + 1], here.at[na + 1, 0]
        up_stage, dn_stage = stage.at[k, 0], stage.at[k, 1]
        no = jnp.logical_not
        return (
            (has_hi_l, has_lo_l, here.at[na, 2 : nb + 1], here.at[0, 2 : nb + 1], (hi_l, me_r), 0, 0),
            (jnp.logical_and(up_dn, no(via_hi)), dn_up, up_ref, up_dst, (hi_l, lo_r), 1, 1),
            (has_lo_l, has_hi_l, here.at[1, 1:nb], here.at[na + 1, 1:nb], (lo_l, me_r), 2, 2),
            (jnp.logical_and(dn_up, no(via_lo)), up_dn, dn_ref, dn_dst, (lo_l, hi_r), 3, 3),
            (has_lo_r, has_hi_r, here.at[2:na, 1], here.at[2:na, nb + 1], (me_l, lo_r), 4, 4),
            (has_hi_r, has_lo_r, here.at[2:na, nb], here.at[2:na, 0], (me_l, hi_r), 5, 5),
            (has_lo_r, has_hi_r, here.at[1, 1], here.at[1, nb + 1], (me_l, lo_r), 6, 6),
            (has_hi_r, has_lo_r, here.at[na, nb], here.at[na, 0], (me_l, hi_r), 7, 7),
            (via_hi, relay_dn, up_ref, up_stage, (me_l + 2, me_r), 1, 8),
            (via_lo, relay_up, dn_ref, dn_stage, (me_l - 2, me_r), 3, 9),
            (relay_dn, None, up_stage, up_dst, (lo_l, lo_r), 8, 1),
            (relay_up, None, dn_stage, dn_dst, (hi_l, hi_r), 9, 3),
        )

    def copy(k, n):
        _, _, src, dst, target, ssem, rsem = hops(k)[n]
        return pltpu.make_async_remote_copy(
            src_ref=src, dst_ref=dst,
            send_sem=send_sem.at[k, ssem], recv_sem=recv_sem.at[k, rsem],
            device_id=target, device_id_type=MESH,
        )

    def send(k, which):
        for n in which:
            pl.when(hops(k)[n][0])(lambda n=n: copy(k, n).start())

    def receive(k, which):
        for n in which:
            pl.when(hops(k)[n][1])(lambda n=n: copy(k, n).wait_recv())

    def forward(k):
        receive(k, (8, 9))
        send(k, (10, 11))

    def clear(missing, slots):
        @pl.when(jnp.logical_not(missing))
        def _():
            for k in range(ITERS):
                for i, j in slots:
                    q[k, i, j] = jnp.zeros((size, size), q.dtype)

    clear(has_lo_l, [(0, j) for j in range(2, nb + 1)])
    clear(dn_up, [(0, nb + 1)])
    clear(has_hi_l, [(na + 1, j) for j in range(1, nb)])
    clear(up_dn, [(na + 1, 0)])
    clear(has_hi_r, [(i, nb + 1) for i in range(1, na)])
    clear(has_lo_r, [(i, 0) for i in range(2, na + 1)])

    local[...] = jnp.zeros(local.shape, jnp.float32)
    partners = nr - 1 + nl - 1
    for other in (up_dn, dn_up, up_up, dn_dn):
        partners = partners + other.astype(jnp.int32)
    loads[0].wait()
    pl.semaphore_wait(barrier, partners)
    send(0, (8, 9, 0, 2, 1, 3, 4, 5, 6, 7))
    loads[1].wait()
    for j in range(nb):
        for t in range(TERMS):
            right_t[j, t] = right[j, t].T
    loads[2].wait()

    def term(i, j, t, source):
        inner = jnp.dot(left[i, t], source, preferred_element_type=jnp.float32)
        return jnp.dot(
            inner.astype(jnp.bfloat16), right_t[j, t], preferred_element_type=jnp.float32
        )

    def gram(i, j, blocks):
        part = jnp.zeros((1, size), jnp.float32)
        for a, b in blocks:
            part += jnp.sum(
                q[i, a + 1, b + 1].astype(jnp.float32) * q[j, a + 1, b + 1].astype(jnp.float32),
                axis=0, keepdims=True,
            )
        row = pl.ds(gram_row(i, j), 1)
        for lane in range(0, size, 128):
            local[row, :] += part[:, lane : lane + 128]

    gram(0, 0, [(a, b) for a in range(na) for b in range(nb)])

    def is_local(t, i, j):
        if t < DIAG:
            return True
        if t < DIAG + HOPS:
            return i >= 1 and j + 1 < nb
        return i + 1 < na and j >= 1

    def offset(t):
        return 0 if t < DIAG else (1 if t < DIAG + HOPS else -1)

    def source_of(k, t, i, j):
        return q[k, i + 1 - offset(t), j + 1 + offset(t)]

    def step(k, carry):
        for i in range(na):
            for j in range(nb):
                own = q[k, i + 1, j + 1]
                total = (energies[j, i] - SHIFT) * own.astype(jnp.float32)
                for t in range(TERMS):
                    if is_local(t, i, j):
                        total += term(i, j, t, source_of(k, t, i, j))
                acc[i, j] = total

        def finish(i, j, ts):
            total = acc[i, j]
            for t in ts:
                total += term(i, j, t, source_of(k, t, i, j))
            acc[i, j] = total
            q[k + 1, i + 1, j + 1] = total.astype(jnp.bfloat16)

        def remote(i, j):
            return [t for t in range(DIAG, TERMS) if not is_local(t, i, j)]

        def grams(blocks):
            lax.fori_loop(0, k + 2, lambda i, c: (gram(i, k + 1, blocks), c)[1], 0)

        def onward(which):
            pl.when(k + 1 < ITERS)(lambda: send(k + 1, which))

        forward(k)
        receive(k, (4, 5, 6, 7))
        for i in range(1, na - 1):
            for j in range(nb):
                finish(i, j, remote(i, j))
        onward((4, 5))
        grams([(i, j) for i in range(1, na - 1) for j in range(nb)])
        receive(k, (0,))
        for j in range(nb - 1):
            finish(0, j, remote(0, j))
        onward((2, 6))
        receive(k, (2,))
        for j in range(1, nb):
            finish(na - 1, j, remote(na - 1, j))
        onward((0, 7))
        grams([(0, j) for j in range(nb - 1)] + [(na - 1, j) for j in range(1, nb)])
        receive(k, (1,))
        finish(0, nb - 1, remote(0, nb - 1))
        onward((9, 3))
        receive(k, (3,))
        finish(na - 1, 0, remote(na - 1, 0))
        onward((8, 1))

        grams([(0, nb - 1), (na - 1, 0)])
        return carry

    lax.fori_loop(0, ITERS, step, 0)

    def spread(slots, me, parts, to, ssem, rsem):
        def copy(n, slot):
            return pltpu.make_async_remote_copy(
                src_ref=slots.at[slot], dst_ref=slots.at[slot],
                send_sem=ssem.at[n], recv_sem=rsem.at[slot],
                device_id=to(lax.rem(me + n, parts)), device_id_type=MESH,
            )

        for n in range(1, parts):
            copy(n, me).start()
        for n in range(1, parts):
            copy(n, lax.rem(me + n, parts)).wait_recv()
        for n in range(1, parts):
            copy(n, me).wait_send()
        total = slots[0]
        for n in range(1, parts):
            total = total + slots[n]
        return total

    totals = jnp.sum(local[...], axis=1, keepdims=True)
    place = lax.broadcasted_iota(jnp.int32, local.shape, 0)
    lanes = lax.broadcasted_iota(jnp.int32, local.shape, 1)
    rows[me_r] = jnp.sum(jnp.where(place == lanes, totals, 0.0), axis=0, keepdims=True)
    cols[me_l] = spread(rows, me_r, nr, lambda r: (me_l, r), rsend, rrecv)
    sums = spread(cols, me_l, nl, lambda l: (l, me_r), csend, crecv)
    sums = sums * count

    def mean(i, j):
        row = gram_row(min(i, j), max(i, j))
        return sums[:, row : row + 1]

    def product(x, y):
        total = jnp.zeros((1, 1), jnp.float32)
        for i in range(ITERS + 1):
            for j in range(ITERS + 1):
                if x[i] is not None and y[j] is not None:
                    total = total + x[i] * y[j] * mean(i, j)
        return total

    def plus(x, y):
        return y if x is None else (x if y is None else x + y)

    def scaled(s, x):
        return [None if part is None else s * part for part in x]

    def combine(*lists):
        return [functools.reduce(plus, parts) for parts in zip(*lists)]

    vec = [lax.rsqrt(mean(0, 0) + eps)] + [None] * ITERS
    previous = [None] * (ITERS + 1)
    for k in range(ITERS):
        sigma = combine([None] + vec[:-1], scaled(SHIFT, vec))
        theta = product(vec, sigma)
        resid = combine(sigma, scaled(-theta, vec))
        if k > 0:
            coef = jnp.full((1, 1), coef_num[k - 1].astype(jnp.float32)) / jnp.full(
                (1, 1), coef_den[k - 1].astype(jnp.float32)
            )
            resid = combine(resid, scaled(-coef, previous))
        ritz[k] = theta[0, 0]
        previous = vec
        vec = scaled(lax.rsqrt(product(resid, resid) + eps), resid)

    stores = []
    for i in range(na):
        for j in range(nb):
            total = acc[i, j] * vec[ITERS]
            for n in range(ITERS):
                total += q[n, i + 1, j + 1].astype(jnp.float32) * vec[n]
            out_v[i, j] = total.astype(jnp.bfloat16)
        stores.append(pltpu.make_async_copy(out_v.at[i], out_hbm.at[i], in_sem.at[i]))
        stores[-1].start()

    for k in range(ITERS):
        for n in range(12):
            pl.when(hops(k)[n][0])(lambda k=k, n=n: copy(k, n).wait_send())
    for store in stores:
        store.wait()


def per_device(nl, nr, psi, left_env, right_env, energies, coef_num, coef_den):
    na, nb, size, _ = psi.shape
    count = 1.0 / float(psi.size * nl * nr)
    anywhere = pl.BlockSpec(memory_space=pl.ANY)
    smem = pl.BlockSpec(memory_space=pltpu.SMEM)
    dma = pltpu.SemaphoreType.DMA
    return pl.pallas_call(
        functools.partial(kernel, nl, nr, count),
        out_shape=(
            jax.ShapeDtypeStruct(psi.shape, jnp.bfloat16),
            jax.ShapeDtypeStruct((ITERS,), jnp.float32),
        ),
        in_specs=[anywhere] * 3 + [smem] * 3,
        out_specs=(anywhere, smem),
        scratch_shapes=[
            pltpu.VMEM((ITERS + 1, na + 2, nb + 2, size, size), jnp.bfloat16),
            pltpu.VMEM((ITERS, 2, size, size), jnp.bfloat16),
            pltpu.VMEM(left_env.shape, jnp.bfloat16),
            pltpu.VMEM(right_env.shape, jnp.bfloat16),
            pltpu.VMEM(right_env.shape, jnp.bfloat16),
            pltpu.VMEM(psi.shape, jnp.float32),
            pltpu.VMEM(psi.shape, jnp.bfloat16),
            pltpu.VMEM((GRAMS, 128), jnp.float32),
            pltpu.VMEM((nr, 1, 128), jnp.float32),
            pltpu.VMEM((nl, 1, 128), jnp.float32),
            dma((ITERS, 10)),
            dma((ITERS, 10)),
            dma((max(3, na),)),
            dma((nr,)),
            dma((nr,)),
            dma((nl,)),
            dma((nl,)),
        ],
        compiler_params=pltpu.CompilerParams(
            collective_id=0, has_side_effects=True, vmem_limit_bytes=60000000
        ),
    )(psi, left_env, right_env, energies.T, coef_num, coef_den)


def solution(mesh):
    in_specs = (
        P("lsec", "rsec", None, None),
        P("lsec", None, None, None),
        P("rsec", None, None, None),
        P("lsec", "rsec"),
        P(),
        P(),
    )
    out_specs = (P("lsec", "rsec", None, None), P())
    body = functools.partial(per_device, mesh.shape["lsec"], mesh.shape["rsec"])
    return jax.shard_map(
        body, mesh=mesh, in_specs=in_specs, out_specs=out_specs, check_vma=False
    )
```
